512 devices in a mesh: dp: 64 (over z_hi, y, x, core), tensor: 8 (over z_lo).
Axes of the slice: x: 4, y: 4, z: 16 (z_hi: 2, z_lo: 8; z = z_hi * 8 + z_lo), core: 2. Of those that a mesh axis runs over, the one named last changes fastest.
Arguments:
- hidden: bfloat16 [8192, 7168], P('dp'), may hold values from -6 to 6
- norm_gain: bfloat16 [7168], replicated, may hold values from 0.099609375 to 1.8984375
- learner_probe_proj: float32 [7168, 4096], P(('dp', 'tensor')), may hold values from -1 to 1
- learner_lookup_proj: float32 [7168, 1024], P(('dp', 'tensor')), may hold values from -3 to 3
- learner_content_proj: float32 [7168, 1024], P(('dp', 'tensor')), may hold values from -0.0625 to 0.0625
- lengths: int32 [4], replicated, may hold values from 1 to 4096, 8192 in all
Outputs:
- serving_combined: bfloat16 [7168, 6144], P('dp', 'tensor')
- spun_lookup_vectors: bfloat16 [8192, 1024], P('dp', 'tensor')
- content_vectors: bfloat16 [8192, 1024], P('dp', 'tensor')
- attention_mix: bfloat16 [8192, 4096], P('dp', 'tensor')
The draws below stay inside these ranges and needn't reach their ends.
Inputs may be any that keep to these rules, and one draw needn't show every extreme that they name: `lengths`: 4 prompts that fill all 8192 tokens; the longest has exactly 4096 tokens.
All inputs are finite; a program needn't handle non-finite values.
Results may differ from the reference program's by a relative error of at most 0.006.
The reference program's roundings to bfloat16 on the way (of `normed` and `weights`) count: a program that leaves them out, or rounds other values in their place, can miss the bound.
Values may be sent and summed in bfloat16 or wider, within the bound.
A program may use at most 64 MiB of HBM per device.

```python
import math
import jax
import jax.numpy as jnp
import numpy as np
from jax import lax

EMBED_DIM = 7168
SHARED_KV_NUM = 8
QUARTET_SHARE = 4
PER_ATTN_DIM = 128
NDOC = 4
TOKENS = 8192
MAXLEN = 4096


def drawn_probe(key):
    content_entries = jax.random.normal(jax.random.fold_in(key, 11), (EMBED_DIM, SHARED_KV_NUM * QUARTET_SHARE * PER_ATTN_DIM), jnp.float32)
    return jnp.clip(content_entries, -5.0, 5.0) * EMBED_DIM ** (-0.5)


def draw_learner_probe_proj(key, part):
    return drawn_probe(key)


def draw_learner_lookup_proj(key, part):
    gaussian_jitter = jax.random.normal(jax.random.fold_in(key, 23), (EMBED_DIM, SHARED_KV_NUM * PER_ATTN_DIM), jnp.float32)
    gaussian_jitter = jnp.clip(gaussian_jitter, -5.0, 5.0) * EMBED_DIM ** (-0.5)
    return gaussian_jitter


def steps_of(key, dims, pieces, least, largest):
    gain, own = 1.0, jax.random.fold_in(key, 6)
    for position, shards_of in pieces:
        heights = jnp.exp(jax.random.uniform(jax.random.fold_in(own, position), (shards_of,), jnp.float32, least / len(pieces), largest / len(pieces)))
        gain = gain * jnp.repeat(heights, dims[position] // shards_of).reshape([-1 if axis == position else 1 for axis in range(len(dims))])
    return gain


def split_up(count, total, bound, skew):
    portions = [(1 << 20) // math.isqrt(rank ** skew) + 1 for rank in range(2, count + 1)]
    spare, holding = total - bound - (count - 1), [1] * (count - 1)
    while spare > 0:
        free = [i for i in range(count - 1) if holding[i] < bound]
        mass, left = sum([portions[i] for i in free]), spare
        for i in free:
            addition = min(bound - holding[i], max(1, left * portions[i] // mass), spare)
            holding[i] = holding[i] + addition
            spare = spare - addition
    return np.array([bound] + holding)


def ragged(own_key, number_of, total, limit, slope):
    if number_of == 2:
        one = jax.random.randint(own_key, (), max(1, total - limit), min(limit, total - 1) + 1)
        return jnp.stack([one, total - one])
    sizes = jnp.asarray(split_up(number_of, total, limit, slope), jnp.int32)
    couples = (number_of - 1) // 2
    source_of, sink = sizes[1:1 + 2 * couples:2], sizes[2:2 + 2 * couples:2]
    margin = jnp.minimum(source_of - 1, limit - sink)
    passed = jax.random.randint(jax.random.fold_in(own_key, 1), (couples,), 0, 1 << 20) % (margin + 1)
    sizes = sizes.at[1:1 + 2 * couples:2].set(source_of - passed).at[2:2 + 2 * couples:2].set(sink + passed)
    return sizes[jax.random.permutation(jax.random.fold_in(own_key, 2), number_of)]


def gaussian(rng, extent, scale, reach, pieces=(), held_as=jnp.bfloat16):
    gain = steps_of(rng, extent, pieces, -0.22, 0.18) if pieces else 1.0
    drawn = jax.random.normal(rng, extent, jnp.float32) * scale * gain
    return jnp.minimum(jnp.maximum(drawn, -reach), reach).astype(held_as)


def setup_inputs(seed: int = 0) -> dict:
    key_list = jax.random.split(jax.random.key(seed), 7)
    hidden = gaussian(key_list[0], (TOKENS, EMBED_DIM), 1.0, 6.0, ((0, 64),))
    norm_gain = jnp.clip(1.0 + 0.18 * jax.random.normal(key_list[1], (EMBED_DIM,), jnp.float32), 0.099609375, 1.8984375).astype(jnp.bfloat16)
    learner_probe_proj = draw_learner_probe_proj(jax.random.fold_in(key_list[6], 71), 0)
    learner_lookup_proj = draw_learner_lookup_proj(jax.random.fold_in(key_list[6], 71), 0)
    learner_content_proj = gaussian(key_list[4], (EMBED_DIM, SHARED_KV_NUM * PER_ATTN_DIM), EMBED_DIM ** -0.5, 0.0625, ((0, 512),), jnp.float32)
    lengths = ragged(key_list[5], NDOC, TOKENS, MAXLEN, 2).astype(jnp.int32)
    return dict(hidden=hidden, norm_gain=norm_gain, learner_probe_proj=learner_probe_proj, learner_lookup_proj=learner_lookup_proj, learner_content_proj=learner_content_proj, lengths=lengths)


rope_theta = 5000000.0
norm_eps = 1e-05
masked_score = -1e+30

def document_start(lengths, positions):
    ends = jnp.cumsum(lengths).astype(jnp.int32)
    starts = (ends - lengths).astype(jnp.int32)
    inside = (positions[:, None] >= starts[None, :]) & (positions[:, None] < ends[None, :])
    return lax.optimization_barrier(jnp.sum(jnp.where(inside, starts[None, :], 0), axis=1)).astype(jnp.int32)

def spin_pairs(content_entries, shift_amounts):
    half_dim = content_entries.shape[-1] // 2
    inverse = rope_theta ** (-2.0 * jnp.arange(half_dim, dtype=jnp.float32) / content_entries.shape[-1])
    angles = shift_amounts.astype(jnp.float32)[:, None] * inverse[None, :]
    cosine = jnp.cos(angles)[:, None, :]
    sine = jnp.sin(angles)[:, None, :]
    first = content_entries[..., :half_dim]
    second = content_entries[..., half_dim:]
    return jnp.concatenate([first * cosine - second * sine, second * cosine + first * sine], axis=-1)

def reference(hidden, norm_gain, learner_probe_proj, learner_lookup_proj, learner_content_proj, lengths):
    prompt_length = hidden.shape[0]
    widened = hidden.astype(jnp.float32)
    scale = lax.rsqrt(lax.optimization_barrier(jnp.mean(widened * widened, axis=1, keepdims=True)) + norm_eps)
    normed = (widened * scale * norm_gain.astype(jnp.float32)[None, :]).astype(jnp.bfloat16)
    combined_slab = jnp.concatenate([learner_probe_proj.reshape(EMBED_DIM, SHARED_KV_NUM, QUARTET_SHARE * PER_ATTN_DIM), learner_lookup_proj.reshape(EMBED_DIM, SHARED_KV_NUM, PER_ATTN_DIM), learner_content_proj.reshape(EMBED_DIM, SHARED_KV_NUM, PER_ATTN_DIM)], axis=2)
    serving_combined = combined_slab.reshape(EMBED_DIM, SHARED_KV_NUM * (QUARTET_SHARE + 2) * PER_ATTN_DIM).astype(jnp.bfloat16)
    mapped_result = jnp.dot(normed, serving_combined, preferred_element_type=jnp.float32)
    mapped_result = mapped_result.reshape(prompt_length, SHARED_KV_NUM, QUARTET_SHARE + 2, PER_ATTN_DIM)
    positions = jnp.arange(prompt_length, dtype=jnp.int32)
    starts = document_start(lengths, positions)
    shift_amounts = positions - starts
    probe_vectors = spin_pairs(mapped_result[:, :, :QUARTET_SHARE, :].reshape(prompt_length, SHARED_KV_NUM * QUARTET_SHARE, PER_ATTN_DIM), shift_amounts).astype(jnp.bfloat16)
    lookup_streams = spin_pairs(mapped_result[:, :, QUARTET_SHARE, :], shift_amounts).astype(jnp.bfloat16)
    content_streams = mapped_result[:, :, QUARTET_SHARE + 1, :].astype(jnp.bfloat16)
    layer_slab = math.gcd(prompt_length, 512)
    slab_total = prompt_length // layer_slab
    window = min(prompt_length, MAXLEN + layer_slab)
    inv_root = 1.0 / math.sqrt(PER_ATTN_DIM)
    keys_wide = lookup_streams.astype(jnp.float32)
    values_wide = content_streams.astype(jnp.float32)

    def one_block(pair):
        group = pair[0]
        index = pair[1]
        begin = index * layer_slab
        chosen = lax.dynamic_slice_in_dim(probe_vectors, begin, layer_slab, 0)
        chosen = lax.dynamic_slice_in_dim(chosen, group * QUARTET_SHARE, QUARTET_SHARE, 1).astype(jnp.float32)
        key_begin = jnp.maximum(begin + layer_slab - window, 0).astype(jnp.int32)
        group_keys = lax.dynamic_slice_in_dim(lax.dynamic_index_in_dim(keys_wide, group, 1, keepdims=False), key_begin, window, 0)
        group_values = lax.dynamic_slice_in_dim(lax.dynamic_index_in_dim(values_wide, group, 1, keepdims=False), key_begin, window, 0)
        key_index = key_begin + jnp.arange(window, dtype=jnp.int32)
        key_start = lax.dynamic_slice_in_dim(starts, key_begin, window, 0)
        query_index = begin + jnp.arange(layer_slab, dtype=jnp.int32)
        query_start = lax.dynamic_slice_in_dim(starts, begin, layer_slab, 0)
        allowed = (key_start[None, :] == query_start[:, None]) & (key_index[None, :] <= query_index[:, None])
        scores = jnp.einsum('qhd,kd->hqk', chosen, group_keys) * inv_root
        scores = jnp.where(allowed[None], scores, masked_score)
        top = lax.optimization_barrier(jnp.max(scores, axis=2, keepdims=True))
        weights = jnp.where(allowed[None], jnp.exp(scores - top), 0.0)
        total = lax.optimization_barrier(jnp.sum(weights, axis=2, keepdims=True))
        rounded = lax.optimization_barrier(weights.astype(jnp.bfloat16)).astype(jnp.float32)
        result = jnp.einsum('hqk,kd->hqd', rounded, group_values) / total
        return result.astype(jnp.bfloat16)
    cluster_labels = jnp.repeat(jnp.arange(SHARED_KV_NUM, dtype=jnp.int32), slab_total)
    slab_labels = jnp.tile(jnp.arange(slab_total, dtype=jnp.int32), SHARED_KV_NUM)
    outcome_entries = lax.map(one_block, (cluster_labels, slab_labels))
    attention_mix = outcome_entries.reshape(SHARED_KV_NUM, slab_total, QUARTET_SHARE, layer_slab, PER_ATTN_DIM).transpose(1, 3, 0, 2, 4)
    attention_mix = attention_mix.reshape(prompt_length, SHARED_KV_NUM * QUARTET_SHARE * PER_ATTN_DIM)
    spun_lookup_vectors = lookup_streams.reshape(prompt_length, SHARED_KV_NUM * PER_ATTN_DIM)
    content_vectors = content_streams.reshape(prompt_length, SHARED_KV_NUM * PER_ATTN_DIM)
    return (serving_combined, spun_lookup_vectors, content_vectors, attention_mix)
```

```python
import functools
import math

import jax
import jax.numpy as jnp
from jax import lax
from jax.experimental import pallas as pl
from jax.experimental.pallas import tpu as pltpu
from jax.sharding import PartitionSpec as P

SHARED_KV_NUM = 8
QUARTET_SHARE = 4
PER_ATTN_DIM = 128
MAXLEN = 4096

rope_theta = 5000000.0
norm_eps = 1e-05
masked_score = -1e30

RING = 4


def document_start(lengths, positions):
    ends = jnp.cumsum(lengths)
    starts = ends - lengths
    inside = (positions[:, None] >= starts[None, :]) & (positions[:, None] < ends[None, :])
    return jnp.sum(jnp.where(inside, starts[None, :], 0), axis=1)


def spread(source, slot, send_sem, recv_sem):
    me = lax.axis_index("dp")
    core = me % 2
    x = (me // 2) % RING
    y = (me // (2 * RING)) % RING
    z = me // (2 * RING * RING)

    def index(dz, dy, dx, other=False):
        c = 1 - core if other else core
        return ((((z + dz) % 2) * RING + (y + dy + RING) % RING) * RING + (x + dx + RING) % RING) * 2 + c

    def along(half, dz, first, second):
        return index(dz, second, first) if half == 0 else index(dz, first, second)

    sibling = index(0, 0, 0, True)
    antipode = index(1, 0, 0)
    barrier = pltpu.get_barrier_semaphore()
    partners = [index(0, 0, 1), index(0, 0, -1), index(0, 1, 0), index(0, -1, 0), antipode, sibling]
    for partner in partners:
        pl.semaphore_signal(
            barrier, inc=1, device_id={"dp": partner}, device_id_type=pl.DeviceIdType.MESH
        )
    pl.semaphore_wait(barrier, len(partners))

    sent = []

    def push(src, origin, half, target):
        copy = pltpu.make_async_remote_copy(
            src_ref=src,
            dst_ref=slot(origin, half),
            send_sem=send_sem.at[len(sent)],
            recv_sem=recv_sem.at[origin, half],
            device_id={"dp": target},
            device_id_type=pl.DeviceIdType.MESH,
        )
        copy.start()
        sent.append(copy)

    def landed(origin, half):
        there = slot(origin, half)
        pltpu.make_async_copy(there, there, recv_sem.at[origin, half]).wait()

    def forward(src, half, dz, first, second):
        origin = along(half, dz, first, second)
        if second == 0:
            if first == 0:
                push(src, origin, half, along(half, 0, 1, 0))
                push(src, origin, half, along(half, 0, -1, 0))
            if first == -1 and dz == 0:
                push(src, origin, half, along(half, 0, 1, 0))
            if first == 1 and dz == 1:
                push(src, origin, half, along(half, 0, -1, 0))
            push(src, origin, half, along(half, 0, 0, 1))
            push(src, origin, half, along(half, 0, 0, -1))
        upward = (abs(first) + dz) % 2 == 0
        if second == -1 and upward:
            push(src, origin, half, along(half, 0, 0, 1))
        if second == 1 and not upward:
            push(src, origin, half, along(half, 0, 0, -1))
        push(src, origin, half, sibling)

    offsets = [(f, s) for f in (0, -1, 1, 2) for s in (0, -1, 1, 2)]
    offsets.sort(key=lambda pair: abs(pair[0]) + abs(pair[1]))
    for half in range(2):
        push(source(half), me, half, antipode)
    for half in range(2):
        forward(source(half), half, 0, 0, 0)
    for dz in range(2):
        for first, second in offsets:
            if (dz, first, second) == (0, 0, 0):
                continue
            for half in range(2):
                origin = along(half, dz, first, second)
                landed(origin, half)
                forward(slot(origin, half), half, dz, first, second)
    for dz in range(2):
        for first, second in offsets:
            for half in range(2):
                origin = along(half, dz, first, second) + 1 - 2 * core
                landed(origin, half)
    for copy in sent:
        copy.wait_send()


SENDS = 2 * (1 + 2 * (3 + 12 + 16))


def project_kernel(normed_ref, block_ref, cos_ref, sin_ref, q_ref, kv_ref, buf, send_sem, recv_sem):
    rows, width = block_ref.shape
    part = width // 2
    me = lax.axis_index("dp")

    def slot(origin, half):
        return buf.at[half, pl.ds(pl.multiple_of(origin * rows, rows), rows), :]

    def source(half):
        return block_ref.at[:, pl.ds(half * part, part)]

    own = pl.ds(pl.multiple_of(me * rows, rows), rows)
    for half in range(2):
        buf[half, own, :] = block_ref[:, half * part : (half + 1) * part]
    spread(source, slot, send_sem, recv_sem)
    cosine = cos_ref[...]
    sine = sin_ref[...]
    heads = part // PER_ATTN_DIM
    for half in range(2):
        mapped = jnp.dot(normed_ref[...], buf[half], preferred_element_type=jnp.float32)
        for j in range(heads):
            head = half * heads + j
            vec = mapped[:, j * PER_ATTN_DIM : (j + 1) * PER_ATTN_DIM]
            if head <= QUARTET_SHARE:
                vec = vec * cosine + pltpu.roll(vec, PER_ATTN_DIM // 2, 1) * sine
            if head < QUARTET_SHARE:
                q_ref[head] = vec.astype(jnp.bfloat16)
            else:
                kv_ref[head - QUARTET_SHARE] = vec.astype(jnp.bfloat16)


def attend_kernel(q_ref, kv_ref, start_ref, mix_ref, buf, send_sem, recv_sem):
    _, rows, width = kv_ref.shape
    me = lax.axis_index("dp")

    def slot(origin, half):
        return buf.at[half, pl.ds(pl.multiple_of(origin * rows, rows), rows), :]

    def source(half):
        return kv_ref.at[half]

    own = pl.ds(pl.multiple_of(me * rows, rows), rows)
    for half in range(2):
        buf[half, own, :] = kv_ref[half]
    spread(source, slot, send_sem, recv_sem)

    lines = QUARTET_SHARE * rows
    step = 512
    inv_root = 1.0 / math.sqrt(PER_ATTN_DIM)
    queries = q_ref[...].reshape(lines, width)
    q_start = start_ref[...]
    q_index = me * rows + lax.broadcasted_iota(jnp.int32, (lines, 1), 0) % rows
    back = MAXLEN // rows
    low = (jnp.maximum(me - back, 0) * rows) // step
    high = ((me + 1) * rows + step - 1) // step

    def one_step(turn, state):
        top, total, accum = state
        begin = pl.multiple_of(turn * step, step)
        keys = buf[0, pl.ds(begin, step), :]
        values = buf[1, pl.ds(begin, step), :]
        key_index = begin + lax.broadcasted_iota(jnp.int32, (1, step), 1)
        allowed = (key_index <= q_index) & (key_index >= q_start)
        scores = (
            lax.dot_general(
                queries, keys, (((1,), (1,)), ((), ())), preferred_element_type=jnp.float32
            )
            * inv_root
        )
        scores = jnp.where(allowed, scores, masked_score)
        new_top = jnp.maximum(top, jnp.max(scores, axis=1, keepdims=True))
        weights = jnp.where(allowed, jnp.exp(scores - new_top), 0.0)
        fade = jnp.exp(top - new_top)
        total = total * fade + jnp.sum(weights, axis=1, keepdims=True)
        accum = accum * fade + jnp.dot(
            weights.astype(jnp.bfloat16), values, preferred_element_type=jnp.float32
        )
        return new_top, total, accum

    initial = (
        jnp.full((lines, 1), masked_score, jnp.float32),
        jnp.zeros((lines, 1), jnp.float32),
        jnp.zeros((lines, width), jnp.float32),
    )
    top, total, accum = lax.fori_loop(low, high, one_step, initial)
    mix = (accum / total).astype(jnp.bfloat16)
    for j in range(QUARTET_SHARE):
        mix_ref[:, j * width : (j + 1) * width] = mix[j * rows : (j + 1) * rows]


def per_device(
    hidden, norm_gain, learner_probe_proj, learner_lookup_proj, learner_content_proj, lengths
):
    tok_rows = hidden.shape[0]
    learner_lines = learner_probe_proj.shape[0]
    group_width = (QUARTET_SHARE + 2) * PER_ATTN_DIM
    combined_slab = jnp.concatenate(
        [
            learner_probe_proj.reshape(learner_lines, SHARED_KV_NUM, QUARTET_SHARE * PER_ATTN_DIM),
            learner_lookup_proj.reshape(learner_lines, SHARED_KV_NUM, PER_ATTN_DIM),
            learner_content_proj.reshape(learner_lines, SHARED_KV_NUM, PER_ATTN_DIM),
        ],
        axis=2,
    )
    combined_slab = combined_slab.reshape(learner_lines, SHARED_KV_NUM * group_width).astype(
        jnp.bfloat16
    )
    serving_combined = lax.all_to_all(
        combined_slab, "tensor", split_axis=1, concat_axis=0, tiled=True
    )
    widened = hidden.astype(jnp.float32)
    scale = lax.rsqrt(jnp.mean(widened * widened, axis=1, keepdims=True) + norm_eps)
    normed = (widened * scale * norm_gain.astype(jnp.float32)[None, :]).astype(jnp.bfloat16)

    my_index = lax.axis_index("dp") * tok_rows + jnp.arange(tok_rows, dtype=jnp.int32)
    my_start = document_start(lengths, my_index)
    half_dim = PER_ATTN_DIM // 2
    inverse = rope_theta ** (-2.0 * jnp.arange(half_dim, dtype=jnp.float32) / PER_ATTN_DIM)
    angles = (my_index - my_start).astype(jnp.float32)[:, None] * inverse[None, :]
    cosine = jnp.cos(angles)
    sine = jnp.sin(angles)
    cosine = jnp.concatenate([cosine, cosine], axis=1)
    sine = jnp.concatenate([-sine, sine], axis=1)

    rows = serving_combined.shape[0]
    devices = 64
    vmem = pl.BlockSpec(memory_space=pltpu.VMEM)
    semaphores = [pltpu.SemaphoreType.DMA((SENDS,)), pltpu.SemaphoreType.DMA((devices, 2))]
    queries, keys_values = pl.pallas_call(
        project_kernel,
        out_shape=(
            jax.ShapeDtypeStruct((QUARTET_SHARE, tok_rows, PER_ATTN_DIM), jnp.bfloat16),
            jax.ShapeDtypeStruct((2, tok_rows, PER_ATTN_DIM), jnp.bfloat16),
        ),
        in_specs=[vmem] * 4,
        out_specs=(vmem, vmem),
        scratch_shapes=[pltpu.VMEM((2, rows * devices, group_width // 2), jnp.bfloat16)]
        + semaphores,
        compiler_params=pltpu.CompilerParams(
            collective_id=0, has_side_effects=True, vmem_limit_bytes=48 * 2**20
        ),
        name="project",
    )(normed, serving_combined, cosine, sine)
    starts = jnp.tile(my_start, QUARTET_SHARE)[:, None]
    attention_mix = pl.pallas_call(
        attend_kernel,
        out_shape=jax.ShapeDtypeStruct((tok_rows, QUARTET_SHARE * PER_ATTN_DIM), jnp.bfloat16),
        in_specs=[vmem] * 3,
        out_specs=vmem,
        scratch_shapes=[pltpu.VMEM((2, tok_rows * devices, PER_ATTN_DIM), jnp.bfloat16)]
        + semaphores,
        compiler_params=pltpu.CompilerParams(
            collective_id=1, has_side_effects=True, vmem_limit_bytes=48 * 2**20
        ),
        name="attend",
    )(queries, keys_values, starts)
    return (serving_combined, keys_values[0], keys_values[1], attention_mix)


def solution(mesh):
    in_specs = (
        P("dp", None),
        P(),
        P(("dp", "tensor"), None),
        P(("dp", "tensor"), None),
        P(("dp", "tensor"), None),
        P(),
    )
    out_specs = (P("dp", "tensor"), P("dp", "tensor"), P("dp", "tensor"), P("dp", "tensor"))
    return jax.shard_map(
        per_device, mesh=mesh, in_specs=in_specs, out_specs=out_specs, check_vma=False
    )
```

```python
import math

import jax
import jax.numpy as jnp
from jax import lax
from jax.experimental import pallas as pl
from jax.experimental.pallas import tpu as pltpu
from jax.sharding import PartitionSpec as P

SHARED_KV_NUM = 8
QUARTET_SHARE = 4
PER_ATTN_DIM = 128
MAXLEN = 4096

rope_theta = 5000000.0
norm_eps = 1e-05
masked_score = -1e30

RING = 4


def document_start(lengths, positions):
    ends = jnp.cumsum(lengths)
    starts = ends - lengths
    inside = (positions[:, None] >= starts[None, :]) & (positions[:, None] < ends[None, :])
    return jnp.sum(jnp.where(inside, starts[None, :], 0), axis=1)


def neighbour_index(dz=0, dy=0, dx=0, other=False):
    me = lax.axis_index("dp")
    core = 1 - me % 2 if other else me % 2
    x = (me // 2) % RING
    y = (me // (2 * RING)) % RING
    z = me // (2 * RING * RING)
    return ((((z + dz) % 2) * RING + (y + dy + RING) % RING) * RING + (x + dx + RING) % RING) * 2 + core


def z_chip(shift):
    plane = 2 * RING * RING
    me = lax.axis_index("dp")
    place = (me // plane) * SHARED_KV_NUM + lax.axis_index("tensor") + shift
    place = (place + 2 * SHARED_KV_NUM) % (2 * SHARED_KV_NUM)
    return (place // SHARED_KV_NUM) * plane + me % plane, place % SHARED_KV_NUM


def greet():
    barrier = pltpu.get_barrier_semaphore()
    tensor = lax.axis_index("tensor")
    partners = [
        (neighbour_index(0, 0, 1), tensor),
        (neighbour_index(0, 0, -1), tensor),
        (neighbour_index(0, 1, 0), tensor),
        (neighbour_index(0, -1, 0), tensor),
        (neighbour_index(0, 0, 0, True), tensor),
        z_chip(Z_STEP),
        z_chip(-Z_STEP),
    ]
    for partner in partners:
        pl.semaphore_signal(
            barrier, inc=1, device_id=partner, device_id_type=pl.DeviceIdType.MESH
        )
    pl.semaphore_wait(barrier, len(partners))


def spread(source, slot, relay, send_sem, recv_sem, relay_sem, started=None, middle=None):
    me = lax.axis_index("dp")
    core = me % 2
    tensor = lax.axis_index("tensor")
    index = neighbour_index

    def along(half, dz, first, second):
        return index(dz, second, first) if half == 0 else index(dz, first, second)

    sibling = index(0, 0, 0, True)
    sent = []

    def push(src, dst, target, arrival):
        copy = pltpu.make_async_remote_copy(
            src_ref=src,
            dst_ref=dst,
            send_sem=send_sem.at[len(sent)],
            recv_sem=arrival,
            device_id=target,
            device_id_type=pl.DeviceIdType.MESH,
        )
        copy.start()
        sent.append(copy)

    def landed(there, arrival):
        pltpu.make_async_copy(there, there, arrival).wait()

    def forward(src, half, dz, first, second):
        origin = along(half, dz, first, second)

        def give(dfirst, dsecond):
            target = (along(half, 0, dfirst, dsecond), tensor)
            push(src, slot(origin, half), target, recv_sem.at[origin, half])

        if second == 0:
            if first == 0:
                give(1, 0)
                give(-1, 0)
            if first == -1 and dz == 0:
                give(1, 0)
            if first == 1 and dz == 1:
                give(-1, 0)
            give(0, 1)
            give(0, -1)
        upward = (abs(first) + dz) % 2 == 0
        if second == -1 and upward:
            give(0, 1)
        if second == 1 and not upward:
            give(0, -1)
        push(src, slot(origin, half), (sibling, tensor), recv_sem.at[origin, half])

    offsets = [(f, s) for f in (0, -1, 1, 2) for s in (0, -1, 1, 2)]
    offsets.sort(key=lambda pair: abs(pair[0]) + abs(pair[1]))

    def receive(dz, hops):
        for first, second in offsets:
            if abs(first) + abs(second) == hops:
                for half in range(2):
                    origin = along(half, dz, first, second)
                    landed(slot(origin, half), recv_sem.at[origin, half])
                    forward(slot(origin, half), half, dz, first, second)

    def from_sibling(dz):
        for first, second in offsets:
            for half in range(2):
                origin = along(half, dz, first, second) + 1 - 2 * core
                landed(slot(origin, half), recv_sem.at[origin, half])

    for half in range(2):
        push(source(half), relay.at[half], z_chip(Z_STEP - 2 * Z_STEP * half), relay_sem.at[half])
    for half in range(2):
        forward(source(half), half, 0, 0, 0)
    if started is not None:
        started()
    receive(0, 1)
    for half in range(2):
        shift = Z_STEP - 2 * Z_STEP * half
        origin, _ = z_chip(-shift)
        landed(relay.at[half], relay_sem.at[half])
        push(relay.at[half], slot(origin, half), z_chip(shift), recv_sem.at[origin, half])
    for hops in range(2, 5):
        receive(0, hops)
    if middle is not None:
        from_sibling(0)
        middle()
    for hops in range(5):
        receive(1, hops)
    if middle is None:
        from_sibling(0)
    from_sibling(1)
    for copy in sent:
        copy.wait_send()


Z_STEP = 4
SENDS = 2 * (2 + 2 * (3 + 12 + 16))


def layer_kernel(
    normed_ref, block_ref, cos_ref, sin_ref, start_ref, kv_ref, mix_ref,
    weights, landing, both, landing_kv, queries, mapped,
    send_sem, recv_sem, relay_sem, send_kv, recv_kv, relay_kv,
):
    lines, width = block_ref.shape
    part = width // 2
    rows = kv_ref.shape[1]
    dim = PER_ATTN_DIM
    me = lax.axis_index("dp")
    heads = part // dim

    greet()

    def slot(origin, half):
        return weights.at[half, pl.ds(pl.multiple_of(origin * lines, lines), lines), :]

    own = pl.ds(pl.multiple_of(me * lines, lines), lines)
    for half in range(2):
        weights[half, own, :] = block_ref[:, half * part : (half + 1) * part]

    reach = normed_ref.shape[1] // 2

    def product(half, plane):
        place = pl.ds(pl.multiple_of(plane * reach, reach), reach)
        return jnp.dot(
            normed_ref[:, place], weights[half, place, :], preferred_element_type=jnp.float32
        )

    plane = me // (2 * RING * RING)

    def near():
        for half in range(2):
            mapped[half] = product(half, plane)

    spread(
        lambda half: block_ref.at[:, pl.ds(half * part, part)],
        slot, landing, send_sem, recv_sem, relay_sem, middle=near,
    )

    def kv_slot(origin, half):
        return both.at[half, pl.ds(pl.multiple_of(origin * rows, rows), rows), :]

    mine = pl.ds(pl.multiple_of(me * rows, rows), rows)

    def finish(half):
        result = mapped[half] + product(half, 1 - plane)
        for j in range(heads):
            head = half * heads + j
            vec = result[:, j * dim : (j + 1) * dim]
            if head <= QUARTET_SHARE:
                vec = vec * cos_ref[...] + pltpu.roll(vec, dim // 2, 1) * sin_ref[...]
            vec = vec.astype(jnp.bfloat16)
            if head < QUARTET_SHARE:
                queries[head * rows : (head + 1) * rows, :] = vec
            else:
                kv_ref[head - QUARTET_SHARE] = vec
                both[head - QUARTET_SHARE, mine, :] = vec

    finish(1)
    spread(
        lambda half: kv_ref.at[half],
        kv_slot, landing_kv, send_kv, recv_kv, relay_kv, started=lambda: finish(0),
    )

    step = 512
    inv_root = 1.0 / math.sqrt(dim)
    total_rows = QUARTET_SHARE * rows
    q = queries[...]
    q_start = start_ref[...]
    q_index = me * rows + lax.broadcasted_iota(jnp.int32, (total_rows, 1), 0) % rows
    back = MAXLEN // rows
    low = (jnp.maximum(me - back, 0) * rows) // step
    high = ((me + 1) * rows + step - 1) // step

    def one_step(turn, state):
        top, total, accum = state
        begin = pl.multiple_of(turn * step, step)
        keys = both[0, pl.ds(begin, step), :]
        values = both[1, pl.ds(begin, step), :]
        key_index = begin + lax.broadcasted_iota(jnp.int32, (1, step), 1)
        allowed = (key_index <= q_index) & (key_index >= q_start)
        scores = (
            lax.dot_general(
                q, keys, (((1,), (1,)), ((), ())), preferred_element_type=jnp.float32
            )
            * inv_root
        )
        scores = jnp.where(allowed, scores, masked_score)
        new_top = jnp.maximum(top, jnp.max(scores, axis=1, keepdims=True))
        weight = jnp.where(allowed, jnp.exp(scores - new_top), 0.0)
        fade = jnp.exp(top - new_top)
        total = total * fade + jnp.sum(weight, axis=1, keepdims=True)
        accum = accum * fade + jnp.dot(
            weight.astype(jnp.bfloat16), values, preferred_element_type=jnp.float32
        )
        return new_top, total, accum

    initial = (
        jnp.full((total_rows, 1), masked_score, jnp.float32),
        jnp.zeros((total_rows, 1), jnp.float32),
        jnp.zeros((total_rows, dim), jnp.float32),
    )
    top, total, accum = lax.fori_loop(low, high, one_step, initial)
    mix = (accum / total).astype(jnp.bfloat16)
    for j in range(QUARTET_SHARE):
        mix_ref[:, j * dim : (j + 1) * dim] = mix[j * rows : (j + 1) * rows]


def per_device(
    hidden, norm_gain, learner_probe_proj, learner_lookup_proj, learner_content_proj, lengths
):
    tok_rows = hidden.shape[0]
    learner_lines = learner_probe_proj.shape[0]
    group_width = (QUARTET_SHARE + 2) * PER_ATTN_DIM
    combined_slab = jnp.concatenate(
        [
            learner_probe_proj.reshape(learner_lines, SHARED_KV_NUM, QUARTET_SHARE * PER_ATTN_DIM),
            learner_lookup_proj.reshape(learner_lines, SHARED_KV_NUM, PER_ATTN_DIM),
            learner_content_proj.reshape(learner_lines, SHARED_KV_NUM, PER_ATTN_DIM),
        ],
        axis=2,
    )
    combined_slab = combined_slab.reshape(learner_lines, SHARED_KV_NUM * group_width).astype(
        jnp.bfloat16
    )
    serving_combined = lax.all_to_all(
        combined_slab, "tensor", split_axis=1, concat_axis=0, tiled=True
    )
    widened = hidden.astype(jnp.float32)
    scale = lax.rsqrt(jnp.mean(widened * widened, axis=1, keepdims=True) + norm_eps)
    normed = (widened * scale * norm_gain.astype(jnp.float32)[None, :]).astype(jnp.bfloat16)

    my_index = lax.axis_index("dp") * tok_rows + jnp.arange(tok_rows, dtype=jnp.int32)
    my_start = document_start(lengths, my_index)
    half_dim = PER_ATTN_DIM // 2
    inverse = rope_theta ** (-2.0 * jnp.arange(half_dim, dtype=jnp.float32) / PER_ATTN_DIM)
    angles = (my_index - my_start).astype(jnp.float32)[:, None] * inverse[None, :]
    cosine = jnp.cos(angles)
    sine = jnp.sin(angles)
    cosine = jnp.concatenate([cosine, cosine], axis=1)
    sine = jnp.concatenate([-sine, sine], axis=1)

    rows = serving_combined.shape[0]
    devices = 4 * RING * RING
    part = group_width // 2
    starts = jnp.tile(my_start, QUARTET_SHARE)[:, None]
    vmem = pl.BlockSpec(memory_space=pltpu.VMEM)
    semaphores = [
        pltpu.SemaphoreType.DMA((SENDS,)),
        pltpu.SemaphoreType.DMA((devices, 2)),
        pltpu.SemaphoreType.DMA((2,)),
    ]
    keys_values, attention_mix = pl.pallas_call(
        layer_kernel,
        out_shape=(
            jax.ShapeDtypeStruct((2, tok_rows, PER_ATTN_DIM), jnp.bfloat16),
            jax.ShapeDtypeStruct((tok_rows, QUARTET_SHARE * PER_ATTN_DIM), jnp.bfloat16),
        ),
        in_specs=[vmem] * 5,
        out_specs=(vmem, vmem),
        scratch_shapes=[
            pltpu.VMEM((2, rows * devices, part), jnp.bfloat16),
            pltpu.VMEM((2, rows, part), jnp.bfloat16),
            pltpu.VMEM((2, tok_rows * devices, PER_ATTN_DIM), jnp.bfloat16),
            pltpu.VMEM((2, tok_rows, PER_ATTN_DIM), jnp.bfloat16),
            pltpu.VMEM((QUARTET_SHARE * tok_rows, PER_ATTN_DIM), jnp.bfloat16),
            pltpu.VMEM((2, tok_rows, part), jnp.float32),
        ]
        + semaphores
        + semaphores,
        compiler_params=pltpu.CompilerParams(
            collective_id=0, has_side_effects=True, vmem_limit_bytes=48 * 2**20
        ),
        name="layer",
    )(normed, serving_combined, cosine, sine, starts)
    return (serving_combined, keys_values[0], keys_values[1], attention_mix)


def solution(mesh):
    in_specs = (
        P("dp", None),
        P(),
        P(("dp", "tensor"), None),
        P(("dp", "tensor"), None),
        P(("dp", "tensor"), None),
        P(),
    )
    out_specs = (P("dp", "tensor"), P("dp", "tensor"), P("dp", "tensor"), P("dp", "tensor"))
    return jax.shard_map(
        per_device, mesh=mesh, in_specs=in_specs, out_specs=out_specs, check_vma=False
    )
```

```python
import math

import jax
import jax.numpy as jnp
from jax import lax
from jax.experimental import pallas as pl
from jax.experimental.pallas import tpu as pltpu
from jax.sharding import PartitionSpec as P

SHARED_KV_NUM = 8
QUARTET_SHARE = 4
PER_ATTN_DIM = 128
MAXLEN = 4096

rope_theta = 5000000.0
norm_eps = 1e-05
masked_score = -1e30

RING = 4


def document_start(lengths, positions):
    ends = jnp.cumsum(lengths)
    starts = ends - lengths
    inside = (positions[:, None] >= starts[None, :]) & (positions[:, None] < ends[None, :])
    return jnp.sum(jnp.where(inside, starts[None, :], 0), axis=1)


def neighbour_index(dz=0, dy=0, dx=0, other=False):
    me = lax.axis_index("dp")
    core = 1 - me % 2 if other else me % 2
    x = (me // 2) % RING
    y = (me // (2 * RING)) % RING
    z = me // (2 * RING * RING)
    return ((((z + dz) % 2) * RING + (y + dy + RING) % RING) * RING + (x + dx + RING) % RING) * 2 + core


def z_chip(shift):
    plane = 2 * RING * RING
    me = lax.axis_index("dp")
    place = (me // plane) * SHARED_KV_NUM + lax.axis_index("tensor") + shift
    place = (place + 2 * SHARED_KV_NUM) % (2 * SHARED_KV_NUM)
    return (place // SHARED_KV_NUM) * plane + me % plane, place % SHARED_KV_NUM


def greet():
    barrier = pltpu.get_barrier_semaphore()
    tensor = lax.axis_index("tensor")
    partners = [
        (neighbour_index(0, 0, 1), tensor),
        (neighbour_index(0, 0, -1), tensor),
        (neighbour_index(0, 1, 0), tensor),
        (neighbour_index(0, -1, 0), tensor),
        (neighbour_index(0, 0, 0, True), tensor),
        z_chip(Z_STEP),
        z_chip(-Z_STEP),
    ]
    for partner in partners:
        pl.semaphore_signal(
            barrier, inc=1, device_id=partner, device_id_type=pl.DeviceIdType.MESH
        )
    pl.semaphore_wait(barrier, len(partners))


def spread(source, slot, relay, send_sem, recv_sem, relay_sem, share=True, middle=None):
    me = lax.axis_index("dp")
    core = me % 2
    tensor = lax.axis_index("tensor")
    index = neighbour_index

    def along(half, dz, first, second):
        return index(dz, second, first) if half == 0 else index(dz, first, second)

    sibling = index(0, 0, 0, True)
    sent = []

    def push(src, dst, target, arrival):
        copy = pltpu.make_async_remote_copy(
            src_ref=src,
            dst_ref=dst,
            send_sem=send_sem.at[len(sent)],
            recv_sem=arrival,
            device_id=target,
            device_id_type=pl.DeviceIdType.MESH,
        )
        copy.start()
        sent.append(copy)

    def landed(there, arrival):
        pltpu.make_async_copy(there, there, arrival).wait()

    def forward(src, half, dz, first, second):
        origin = along(half, dz, first, second)

        def give(dfirst, dsecond):
            target = (along(half, 0, dfirst, dsecond), tensor)
            push(src, slot(origin, half), target, recv_sem.at[origin, half])

        if second == 0:
            if first == 0:
                give(1, 0)
                give(-1, 0)
            if first == -1 and dz == 0:
                give(1, 0)
            if first == 1 and dz == 1:
                give(-1, 0)
            give(0, 1)
            give(0, -1)
        upward = (abs(first) + dz) % 2 == 0
        if second == -1 and upward:
            give(0, 1)
        if second == 1 and not upward:
            give(0, -1)
        if share:
            push(src, slot(origin, half), (sibling, tensor), recv_sem.at[origin, half])

    offsets = [(f, s) for f in (0, -1, 1, 2) for s in (0, -1, 1, 2)]
    offsets.sort(key=lambda pair: abs(pair[0]) + abs(pair[1]))

    def receive(dz, hops):
        for first, second in offsets:
            if abs(first) + abs(second) == hops:
                for half in range(2):
                    origin = along(half, dz, first, second)
                    landed(slot(origin, half), recv_sem.at[origin, half])
                    forward(slot(origin, half), half, dz, first, second)

    def from_sibling(dz):
        for first, second in offsets:
            for half in range(2):
                origin = along(half, dz, first, second) + 1 - 2 * core
                landed(slot(origin, half), recv_sem.at[origin, half])

    for half in range(2):
        push(source(half), relay.at[half], z_chip(Z_STEP - 2 * Z_STEP * half), relay_sem.at[half])
    for half in range(2):
        forward(source(half), half, 0, 0, 0)
    receive(0, 1)
    for half in range(2):
        shift = Z_STEP - 2 * Z_STEP * half
        origin, _ = z_chip(-shift)
        landed(relay.at[half], relay_sem.at[half])
        push(relay.at[half], slot(origin, half), z_chip(shift), recv_sem.at[origin, half])
    for hops in range(2, 5):
        receive(0, hops)
    if middle is not None:
        middle()
    for hops in range(5):
        receive(1, hops)
    if share:
        from_sibling(0)
        from_sibling(1)
    for copy in sent:
        copy.wait_send()


Z_STEP = 4
SENDS = 2 * (2 + 2 * (3 + 12))
SHARED_SENDS = SENDS + 2 * 2 * 16


def layer_kernel(
    normed_ref, block_ref, cos_ref, sin_ref, start_ref, kv_ref, mix_ref,
    weights, landing, both, landing_kv, tokens, mapped, made, parts,
    send_sem, recv_sem, relay_sem, send_kv, recv_kv, relay_kv, pair_send, pair_recv, local_sem,
):
    lines, width = block_ref.shape
    part = width // 2
    rows = kv_ref.shape[1]
    dim = PER_ATTN_DIM
    me = lax.axis_index("dp")
    core = me % 2
    heads = part // dim

    greet()

    def pair(src, dst, number):
        copy = pltpu.make_async_remote_copy(
            src_ref=src,
            dst_ref=dst,
            send_sem=pair_send.at[number],
            recv_sem=pair_recv.at[number],
            device_id=(neighbour_index(0, 0, 0, True), lax.axis_index("tensor")),
            device_id_type=pl.DeviceIdType.MESH,
        )
        copy.start()
        return copy

    def slot(origin, half):
        row = (origin // 2 * 2 + half) * lines
        return weights.at[pl.ds(pl.multiple_of(row, lines), lines), :]

    own = weights.at[pl.ds(pl.multiple_of(me * lines, lines), lines), :]
    block_swap = pair(
        block_ref.at[:, pl.ds(pl.multiple_of((1 - core) * part, part), part)], own, 0
    )
    keep = pltpu.make_async_copy(
        block_ref.at[:, pl.ds(pl.multiple_of(core * part, part), part)], own, local_sem.at[0]
    )
    keep.start()
    seat = tokens.at[pl.ds(pl.multiple_of(core * rows, rows), rows), :]
    token_swap = pair(normed_ref, seat, 1)
    keep_tokens = pltpu.make_async_copy(normed_ref, seat, local_sem.at[1])
    keep_tokens.start()
    keep.wait()
    block_swap.wait_recv()

    reach = normed_ref.shape[1] // 2
    plane = me // (2 * RING * RING)

    def product(which):
        place = pl.ds(pl.multiple_of(which * reach, reach), reach)
        return jnp.dot(
            tokens[:, place], weights[place, :], preferred_element_type=jnp.float32
        )

    def near():
        keep_tokens.wait()
        token_swap.wait_recv()
        mapped[...] = product(plane)

    spread(
        lambda half: slot(me, half),
        slot, landing, send_sem, recv_sem, relay_sem, share=False, middle=near,
    )
    block_swap.wait_send()
    token_swap.wait_send()

    result = mapped[...] + product(1 - plane)
    for j in range(heads):
        vec = result[:, j * dim : (j + 1) * dim]
        spun = vec * cos_ref[...] + pltpu.roll(vec, dim // 2, 1) * sin_ref[...]
        if j == heads - 1:
            spun = jnp.where(core == 0, spun, vec)
        made[j] = spun.astype(jnp.bfloat16)
    theirs = pl.ds(pl.multiple_of((1 - core) * rows, rows), rows)
    ours = pl.ds(pl.multiple_of(core * rows, rows), rows)
    head_swap = pair(made.at[:, theirs, :], parts.at[pl.ds(core * heads, heads)], 2)
    for j in range(heads):
        parts[core * heads + j] = made[j, ours, :]
    head_swap.wait()

    def kv_slot(origin, half):
        return both.at[half, pl.ds(pl.multiple_of(origin * rows, rows), rows), :]

    mine = pl.ds(pl.multiple_of(me * rows, rows), rows)
    for half in range(2):
        kv_ref[half] = parts[QUARTET_SHARE + half]
        both[half, mine, :] = parts[QUARTET_SHARE + half]
    spread(
        lambda half: parts.at[QUARTET_SHARE + half],
        kv_slot, landing_kv, send_kv, recv_kv, relay_kv,
    )

    step = 512
    inv_root = 1.0 / math.sqrt(dim)
    total_rows = QUARTET_SHARE * rows
    q = parts[:QUARTET_SHARE].reshape(total_rows, dim)
    q_start = start_ref[...]
    q_index = me * rows + lax.broadcasted_iota(jnp.int32, (total_rows, 1), 0) % rows
    back = MAXLEN // rows
    low = (jnp.maximum(me - back, 0) * rows) // step
    high = ((me + 1) * rows + step - 1) // step

    def one_step(turn, state):
        top, total, accum = state
        begin = pl.multiple_of(turn * step, step)
        keys = both[0, pl.ds(begin, step), :]
        values = both[1, pl.ds(begin, step), :]
        key_index = begin + lax.broadcasted_iota(jnp.int32, (1, step), 1)
        allowed = (key_index <= q_index) & (key_index >= q_start)
        scores = (
            lax.dot_general(
                q, keys, (((1,), (1,)), ((), ())), preferred_element_type=jnp.float32
            )
            * inv_root
        )
        scores = jnp.where(allowed, scores, masked_score)
        new_top = jnp.maximum(top, jnp.max(scores, axis=1, keepdims=True))
        weight = jnp.where(allowed, jnp.exp(scores - new_top), 0.0)
        fade = jnp.exp(top - new_top)
        total = total * fade + jnp.sum(weight, axis=1, keepdims=True)
        accum = accum * fade + jnp.dot(
            weight.astype(jnp.bfloat16), values, preferred_element_type=jnp.float32
        )
        return new_top, total, accum

    initial = (
        jnp.full((total_rows, 1), masked_score, jnp.float32),
        jnp.zeros((total_rows, 1), jnp.float32),
        jnp.zeros((total_rows, dim), jnp.float32),
    )
    top, total, accum = lax.fori_loop(low, high, one_step, initial)
    mix = (accum / total).astype(jnp.bfloat16)
    for j in range(QUARTET_SHARE):
        mix_ref[:, j * dim : (j + 1) * dim] = mix[j * rows : (j + 1) * rows]


def per_device(
    hidden, norm_gain, learner_probe_proj, learner_lookup_proj, learner_content_proj, lengths
):
    tok_rows = hidden.shape[0]
    learner_lines = learner_probe_proj.shape[0]
    group_width = (QUARTET_SHARE + 2) * PER_ATTN_DIM
    combined_slab = jnp.concatenate(
        [
            learner_probe_proj.reshape(learner_lines, SHARED_KV_NUM, QUARTET_SHARE * PER_ATTN_DIM),
            learner_lookup_proj.reshape(learner_lines, SHARED_KV_NUM, PER_ATTN_DIM),
            learner_content_proj.reshape(learner_lines, SHARED_KV_NUM, PER_ATTN_DIM),
        ],
        axis=2,
    )
    combined_slab = combined_slab.reshape(learner_lines, SHARED_KV_NUM * group_width).astype(
        jnp.bfloat16
    )
    serving_combined = lax.all_to_all(
        combined_slab, "tensor", split_axis=1, concat_axis=0, tiled=True
    )
    widened = hidden.astype(jnp.float32)
    scale = lax.rsqrt(jnp.mean(widened * widened, axis=1, keepdims=True) + norm_eps)
    normed = (widened * scale * norm_gain.astype(jnp.float32)[None, :]).astype(jnp.bfloat16)

    my_index = lax.axis_index("dp") * tok_rows + jnp.arange(tok_rows, dtype=jnp.int32)
    my_start = document_start(lengths, my_index)
    pair_index = (lax.axis_index("dp") // 2) * 2 * tok_rows + jnp.arange(
        2 * tok_rows, dtype=jnp.int32
    )
    pair_start = document_start(lengths, pair_index)
    half_dim = PER_ATTN_DIM // 2
    inverse = rope_theta ** (-2.0 * jnp.arange(half_dim, dtype=jnp.float32) / PER_ATTN_DIM)
    angles = (pair_index - pair_start).astype(jnp.float32)[:, None] * inverse[None, :]
    cosine = jnp.cos(angles)
    sine = jnp.sin(angles)
    cosine = jnp.concatenate([cosine, cosine], axis=1)
    sine = jnp.concatenate([-sine, sine], axis=1)

    rows = serving_combined.shape[0]
    devices = 4 * RING * RING
    part = group_width // 2
    starts = jnp.tile(my_start, QUARTET_SHARE)[:, None]
    vmem = pl.BlockSpec(memory_space=pltpu.VMEM)
    semaphores = []
    for sends in (SENDS, SHARED_SENDS):
        semaphores += [
            pltpu.SemaphoreType.DMA((sends,)),
            pltpu.SemaphoreType.DMA((devices, 2)),
            pltpu.SemaphoreType.DMA((2,)),
        ]
    semaphores += [
        pltpu.SemaphoreType.DMA((3,)),
        pltpu.SemaphoreType.DMA((3,)),
        pltpu.SemaphoreType.DMA((2,)),
    ]
    keys_values, attention_mix = pl.pallas_call(
        layer_kernel,
        out_shape=(
            jax.ShapeDtypeStruct((2, tok_rows, PER_ATTN_DIM), jnp.bfloat16),
            jax.ShapeDtypeStruct((tok_rows, QUARTET_SHARE * PER_ATTN_DIM), jnp.bfloat16),
        ),
        in_specs=[vmem] * 5,
        out_specs=(vmem, vmem),
        scratch_shapes=[
            pltpu.VMEM((rows * devices, part), jnp.bfloat16),
            pltpu.VMEM((2, rows, part), jnp.bfloat16),
            pltpu.VMEM((2, tok_rows * devices, PER_ATTN_DIM), jnp.bfloat16),
            pltpu.VMEM((2, tok_rows, PER_ATTN_DIM), jnp.bfloat16),
            pltpu.VMEM((2 * tok_rows, hidden.shape[1]), jnp.bfloat16),
            pltpu.VMEM((2 * tok_rows, part), jnp.float32),
            pltpu.VMEM((3, 2 * tok_rows, PER_ATTN_DIM), jnp.bfloat16),
            pltpu.VMEM((6, tok_rows, PER_ATTN_DIM), jnp.bfloat16),
        ]
        + semaphores,
        compiler_params=pltpu.CompilerParams(
            collective_id=0, has_side_effects=True, vmem_limit_bytes=48 * 2**20
        ),
        name="layer",
    )(normed, serving_combined, cosine, sine, starts)
    return (serving_combined, keys_values[0], keys_values[1], attention_mix)


def solution(mesh):
    in_specs = (
        P("dp", None),
        P(),
        P(("dp", "tensor"), None),
        P(("dp", "tensor"), None),
        P(("dp", "tensor"), None),
        P(),
    )
    out_specs = (P("dp", "tensor"), P("dp", "tensor"), P("dp", "tensor"), P("dp", "tensor"))
    return jax.shard_map(
        per_device, mesh=mesh, in_specs=in_specs, out_specs=out_specs, check_vma=False
    )
```

```python
import math

import jax
import jax.numpy as jnp
from jax import lax
from jax.experimental import pallas as pl
from jax.experimental.pallas import tpu as pltpu
from jax.sharding import PartitionSpec as P

SHARED_KV_NUM = 8
QUARTET_SHARE = 4
PER_ATTN_DIM = 128
MAXLEN = 4096

rope_theta = 5000000.0
norm_eps = 1e-05
masked_score = -1e30

RING = 4


def document_start(lengths, positions):
    ends = jnp.cumsum(lengths)
    starts = ends - lengths
    inside = (positions[:, None] >= starts[None, :]) & (positions[:, None] < ends[None, :])
    return jnp.sum(jnp.where(inside, starts[None, :], 0), axis=1)


def neighbour_index(dz=0, dy=0, dx=0, other=False):
    me = lax.axis_index("dp")
    core = 1 - me % 2 if other else me % 2
    x = (me // 2) % RING
    y = (me // (2 * RING)) % RING
    z = me // (2 * RING * RING)
    return ((((z + dz) % 2) * RING + (y + dy + RING) % RING) * RING + (x + dx + RING) % RING) * 2 + core


def z_chip(shift):
    plane = 2 * RING * RING
    me = lax.axis_index("dp")
    place = (me // plane) * SHARED_KV_NUM + lax.axis_index("tensor") + shift
    place = (place + 2 * SHARED_KV_NUM) % (2 * SHARED_KV_NUM)
    return (place // SHARED_KV_NUM) * plane + me % plane, place % SHARED_KV_NUM


def greet():
    barrier = pltpu.get_barrier_semaphore()
    tensor = lax.axis_index("tensor")
    partners = [
        (neighbour_index(0, 0, 1), tensor),
        (neighbour_index(0, 0, -1), tensor),
        (neighbour_index(0, 1, 0), tensor),
        (neighbour_index(0, -1, 0), tensor),
        (neighbour_index(0, 0, 0, True), tensor),
        z_chip(Z_STEP),
        z_chip(-Z_STEP),
    ]
    for partner in partners:
        pl.semaphore_signal(
            barrier, inc=1, device_id=partner, device_id_type=pl.DeviceIdType.MESH
        )
    pl.semaphore_wait(barrier, len(partners))


def spread(source, slot, relay, send_sem, recv_sem, relay_sem, share, middle, after=None):
    me = lax.axis_index("dp")
    core = me % 2
    tensor = lax.axis_index("tensor")
    index = neighbour_index

    def along(half, dz, first, second):
        return index(dz, second, first) if half == 0 else index(dz, first, second)

    sibling = index(0, 0, 0, True)
    sent = []

    def push(src, dst, target, arrival):
        copy = pltpu.make_async_remote_copy(
            src_ref=src,
            dst_ref=dst,
            send_sem=send_sem.at[len(sent)],
            recv_sem=arrival,
            device_id=target,
            device_id_type=pl.DeviceIdType.MESH,
        )
        copy.start()
        sent.append(copy)

    def landed(there, arrival):
        pltpu.make_async_copy(there, there, arrival).wait()

    def forward(src, half, dz, first, second):
        origin = along(half, dz, first, second)

        def give(dfirst, dsecond):
            target = (along(half, 0, dfirst, dsecond), tensor)
            push(src, slot(origin, half), target, recv_sem.at[origin, half])

        if second == 0:
            if first == 0:
                give(1, 0)
                give(-1, 0)
            if first == -1 and dz == 0:
                give(1, 0)
            if first == 1 and dz == 1:
                give(-1, 0)
            give(0, 1)
            give(0, -1)
        upward = (abs(first) + dz) % 2 == 0
        if second == -1 and upward:
            give(0, 1)
        if second == 1 and not upward:
            give(0, -1)
        if share:
            push(src, slot(origin, half), (sibling, tensor), recv_sem.at[origin, half])

    offsets = [(f, s) for f in (0, -1, 1, 2) for s in (0, -1, 1, 2)]
    offsets.sort(key=lambda pair: abs(pair[0]) + abs(pair[1]))

    def receive(dz, hops):
        for first, second in offsets:
            if abs(first) + abs(second) == hops:
                for half in range(2):
                    origin = along(half, dz, first, second)
                    landed(slot(origin, half), recv_sem.at[origin, half])
                    forward(slot(origin, half), half, dz, first, second)

    def from_sibling(dz, lanes=(0, -1, 1, 2)):
        for first, second in offsets:
            for half in range(2):
                if (second if half == 0 else first) not in lanes:
                    continue
                origin = along(half, dz, first, second) + 1 - 2 * core
                landed(slot(origin, half), recv_sem.at[origin, half])

    for half in range(2):
        push(source(half), relay.at[half], z_chip(Z_STEP - 2 * Z_STEP * half), relay_sem.at[half])
    for half in range(2):
        forward(source(half), half, 0, 0, 0)
    receive(0, 1)
    for half in range(2):
        shift = Z_STEP - 2 * Z_STEP * half
        origin, _ = z_chip(-shift)
        landed(relay.at[half], relay_sem.at[half])
        push(relay.at[half], slot(origin, half), z_chip(shift), recv_sem.at[origin, half])
    for hops in range(2, 5):
        receive(0, hops)
    middle(from_sibling)
    for hops in range(5):
        receive(1, hops)
        if after is not None:
            after(hops, from_sibling)
    for copy in sent:
        copy.wait_send()


Z_STEP = 4
SENDS = 2 * (2 + 2 * (3 + 12))
SHARED_SENDS = SENDS + 2 * 2 * 16


def layer_kernel(
    normed_ref, block_ref, cos_ref, sin_ref, start_ref, kv_ref, mix_ref,
    weights, landing, both, landing_kv, tokens, mapped, made, parts,
    send_sem, recv_sem, relay_sem, send_kv, recv_kv, relay_kv, pair_send, pair_recv, local_sem,
):
    lines, width = block_ref.shape
    part = width // 2
    rows = kv_ref.shape[1]
    dim = PER_ATTN_DIM
    me = lax.axis_index("dp")
    core = me % 2
    heads = part // dim

    greet()

    def pair(src, dst, number):
        copy = pltpu.make_async_remote_copy(
            src_ref=src,
            dst_ref=dst,
            send_sem=pair_send.at[number],
            recv_sem=pair_recv.at[number],
            device_id=(neighbour_index(0, 0, 0, True), lax.axis_index("tensor")),
            device_id_type=pl.DeviceIdType.MESH,
        )
        copy.start()
        return copy

    def slot(origin, half):
        row = (origin // 2 * 2 + half) * lines
        return weights.at[pl.ds(pl.multiple_of(row, lines), lines), :]

    own = weights.at[pl.ds(pl.multiple_of(me * lines, lines), lines), :]
    block_swap = pair(
        block_ref.at[:, pl.ds(pl.multiple_of((1 - core) * part, part), part)], own, 0
    )
    keep = pltpu.make_async_copy(
        block_ref.at[:, pl.ds(pl.multiple_of(core * part, part), part)], own, local_sem.at[0]
    )
    keep.start()
    seat = tokens.at[pl.ds(pl.multiple_of(core * rows, rows), rows), :]
    token_swap = pair(normed_ref, seat, 1)
    keep_tokens = pltpu.make_async_copy(normed_ref, seat, local_sem.at[1])
    keep_tokens.start()
    keep.wait()
    block_swap.wait_recv()

    reach = normed_ref.shape[1] // 2
    plane = me // (2 * RING * RING)

    def product(which):
        place = pl.ds(pl.multiple_of(which * reach, reach), reach)
        return jnp.dot(
            tokens[:, place], weights[place, :], preferred_element_type=jnp.float32
        )

    def near(_):
        keep_tokens.wait()
        token_swap.wait_recv()
        mapped[...] = product(plane)

    spread(
        lambda half: slot(me, half),
        slot, landing, send_sem, recv_sem, relay_sem, False, near,
    )
    block_swap.wait_send()
    token_swap.wait_send()

    result = mapped[...] + product(1 - plane)
    for j in range(heads):
        vec = result[:, j * dim : (j + 1) * dim]
        spun = vec * cos_ref[...] + pltpu.roll(vec, dim // 2, 1) * sin_ref[...]
        if j == heads - 1:
            spun = jnp.where(core == 0, spun, vec)
        made[j] = spun.astype(jnp.bfloat16)
    theirs = pl.ds(pl.multiple_of((1 - core) * rows, rows), rows)
    ours = pl.ds(pl.multiple_of(core * rows, rows), rows)
    head_swap = pair(made.at[:, theirs, :], parts.at[pl.ds(core * heads, heads)], 2)
    for j in range(heads):
        parts[core * heads + j] = made[j, ours, :]
    head_swap.wait()

    def kv_slot(origin, half):
        return both.at[half, pl.ds(pl.multiple_of(origin * rows, rows), rows), :]

    mine = pl.ds(pl.multiple_of(me * rows, rows), rows)
    for half in range(2):
        kv_ref[half] = parts[QUARTET_SHARE + half]
        both[half, mine, :] = parts[QUARTET_SHARE + half]
    step = 512
    inv_root = 1.0 / math.sqrt(dim)
    total_rows = QUARTET_SHARE * rows
    q = parts[:QUARTET_SHARE].reshape(total_rows, dim)
    q_start = start_ref[...]
    q_index = me * rows + lax.broadcasted_iota(jnp.int32, (total_rows, 1), 0) % rows
    back = MAXLEN // rows
    low = (jnp.maximum(me - back, 0) * rows) // step
    high = ((me + 1) * rows + step - 1) // step

    def one_step(turn, state):
        top, total, accum = state
        begin = pl.multiple_of(turn * step, step)
        keys = both[0, pl.ds(begin, step), :]
        values = both[1, pl.ds(begin, step), :]
        key_index = begin + lax.broadcasted_iota(jnp.int32, (1, step), 1)
        allowed = (key_index <= q_index) & (key_index >= q_start)
        scores = (
            lax.dot_general(
                q, keys, (((1,), (1,)), ((), ())), preferred_element_type=jnp.float32
            )
            * inv_root
        )
        scores = jnp.where(allowed, scores, masked_score)
        new_top = jnp.maximum(top, jnp.max(scores, axis=1, keepdims=True))
        weight = jnp.exp(scores - new_top)
        fade = jnp.exp(top - new_top)
        total = total * fade + jnp.sum(weight, axis=1, keepdims=True)
        accum = accum * fade + jnp.dot(
            weight.astype(jnp.bfloat16), values, preferred_element_type=jnp.float32
        )
        return new_top, total, accum

    initial = (
        jnp.full((total_rows, 1), masked_score, jnp.float32),
        jnp.zeros((total_rows, 1), jnp.float32),
        jnp.zeros((total_rows, dim), jnp.float32),
    )
    state = [initial]

    def run(begin, end):
        count = jnp.maximum(end - begin, 0)
        state[0] = lax.fori_loop(
            0, count, lambda turn, held: one_step(end - 1 - turn, held), state[0]
        )

    half_steps = MAXLEN // step
    own_low = jnp.maximum(low, half_steps * plane)
    marks = [high] + [jnp.maximum(own_low, high - k) for k in (4, 6, half_steps)]
    y = (me // (2 * RING)) % RING
    row_steps = half_steps // RING

    def far_row(dy):
        first_step = (y + dy + RING) % RING * row_steps
        run(jnp.maximum(first_step, low), jnp.minimum(first_step + row_steps, half_steps * plane))

    def near_keys(from_sibling):
        from_sibling(0)
        run(marks[1], marks[0])

    def far_keys(hops, from_sibling):
        if hops in (1, 2):
            run(marks[hops + 1], marks[hops])
        if hops == 3:
            from_sibling(1, (0,))
            far_row(0)
        if hops == 4:
            from_sibling(1, (-1, 1))
            far_row(-1)
            far_row(1)
            from_sibling(1, (2,))
            far_row(2)

    spread(
        lambda half: parts.at[QUARTET_SHARE + half],
        kv_slot, landing_kv, send_kv, recv_kv, relay_kv, True, near_keys, far_keys,
    )
    top, total, accum = state[0]
    mix = (accum / total).astype(jnp.bfloat16)
    for j in range(QUARTET_SHARE):
        mix_ref[:, j * dim : (j + 1) * dim] = mix[j * rows : (j + 1) * rows]


def per_device(
    hidden, norm_gain, learner_probe_proj, learner_lookup_proj, learner_content_proj, lengths
):
    tok_rows = hidden.shape[0]
    learner_lines = learner_probe_proj.shape[0]
    group_width = (QUARTET_SHARE + 2) * PER_ATTN_DIM
    combined_slab = jnp.concatenate(
        [
            learner_probe_proj.reshape(learner_lines, SHARED_KV_NUM, QUARTET_SHARE * PER_ATTN_DIM),
            learner_lookup_proj.reshape(learner_lines, SHARED_KV_NUM, PER_ATTN_DIM),
            learner_content_proj.reshape(learner_lines, SHARED_KV_NUM, PER_ATTN_DIM),
        ],
        axis=2,
    )
    combined_slab = combined_slab.reshape(learner_lines, SHARED_KV_NUM * group_width).astype(
        jnp.bfloat16
    )
    serving_combined = lax.all_to_all(
        combined_slab, "tensor", split_axis=1, concat_axis=0, tiled=True
    )
    widened = hidden.astype(jnp.float32)
    scale = lax.rsqrt(jnp.mean(widened * widened, axis=1, keepdims=True) + norm_eps)
    normed = (widened * scale * norm_gain.astype(jnp.float32)[None, :]).astype(jnp.bfloat16)

    my_index = lax.axis_index("dp") * tok_rows + jnp.arange(tok_rows, dtype=jnp.int32)
    my_start = document_start(lengths, my_index)
    pair_index = (lax.axis_index("dp") // 2) * 2 * tok_rows + jnp.arange(
        2 * tok_rows, dtype=jnp.int32
    )
    pair_start = document_start(lengths, pair_index)
    half_dim = PER_ATTN_DIM // 2
    inverse = rope_theta ** (-2.0 * jnp.arange(half_dim, dtype=jnp.float32) / PER_ATTN_DIM)
    angles = (pair_index - pair_start).astype(jnp.float32)[:, None] * inverse[None, :]
    cosine = jnp.cos(angles)
    sine = jnp.sin(angles)
    cosine = jnp.concatenate([cosine, cosine], axis=1)
    sine = jnp.concatenate([-sine, sine], axis=1)

    rows = serving_combined.shape[0]
    devices = 4 * RING * RING
    part = group_width // 2
    starts = jnp.tile(my_start, QUARTET_SHARE)[:, None]
    vmem = pl.BlockSpec(memory_space=pltpu.VMEM)
    semaphores = []
    for sends in (SENDS, SHARED_SENDS):
        semaphores += [
            pltpu.SemaphoreType.DMA((sends,)),
            pltpu.SemaphoreType.DMA((devices, 2)),
            pltpu.SemaphoreType.DMA((2,)),
        ]
    semaphores += [
        pltpu.SemaphoreType.DMA((3,)),
        pltpu.SemaphoreType.DMA((3,)),
        pltpu.SemaphoreType.DMA((2,)),
    ]
    keys_values, attention_mix = pl.pallas_call(
        layer_kernel,
        out_shape=(
            jax.ShapeDtypeStruct((2, tok_rows, PER_ATTN_DIM), jnp.bfloat16),
            jax.ShapeDtypeStruct((tok_rows, QUARTET_SHARE * PER_ATTN_DIM), jnp.bfloat16),
        ),
        in_specs=[vmem] * 5,
        out_specs=(vmem, vmem),
        scratch_shapes=[
            pltpu.VMEM((rows * devices, part), jnp.bfloat16),
            pltpu.VMEM((2, rows, part), jnp.bfloat16),
            pltpu.VMEM((2, tok_rows * devices, PER_ATTN_DIM), jnp.bfloat16),
            pltpu.VMEM((2, tok_rows, PER_ATTN_DIM), jnp.bfloat16),
            pltpu.VMEM((2 * tok_rows, hidden.shape[1]), jnp.bfloat16),
            pltpu.VMEM((2 * tok_rows, part), jnp.float32),
            pltpu.VMEM((3, 2 * tok_rows, PER_ATTN_DIM), jnp.bfloat16),
            pltpu.VMEM((6, tok_rows, PER_ATTN_DIM), jnp.bfloat16),
        ]
        + semaphores,
        compiler_params=pltpu.CompilerParams(
            collective_id=0, has_side_effects=True, vmem_limit_bytes=48 * 2**20
        ),
        name="layer",
    )(normed, serving_combined, cosine, sine, starts)
    return (serving_combined, keys_values[0], keys_values[1], attention_mix)


def solution(mesh):
    in_specs = (
        P("dp", None),
        P(),
        P(("dp", "tensor"), None),
        P(("dp", "tensor"), None),
        P(("dp", "tensor"), None),
        P(),
    )
    out_specs = (P("dp", "tensor"), P("dp", "tensor"), P("dp", "tensor"), P("dp", "tensor"))
    return jax.shard_map(
        per_device, mesh=mesh, in_specs=in_specs, out_specs=out_specs, check_vma=False
    )
```

```python
import math

import jax
import jax.numpy as jnp
from jax import lax
from jax.experimental import pallas as pl
from jax.experimental.pallas import tpu as pltpu
from jax.sharding import PartitionSpec as P

SHARED_KV_NUM = 8
QUARTET_SHARE = 4
PER_ATTN_DIM = 128
MAXLEN = 4096

rope_theta = 5000000.0
norm_eps = 1e-05
masked_score = -1e30

RING = 4


def document_start(lengths, positions):
    ends = jnp.cumsum(lengths)
    starts = ends - lengths
    inside = (positions[:, None] >= starts[None, :]) & (positions[:, None] < ends[None, :])
    return jnp.sum(jnp.where(inside, starts[None, :], 0), axis=1)


def neighbour_index(dz=0, dy=0, dx=0, other=False):
    me = lax.axis_index("dp")
    core = 1 - me % 2 if other else me % 2
    x = (me // 2) % RING
    y = (me // (2 * RING)) % RING
    z = me // (2 * RING * RING)
    return ((((z + dz) % 2) * RING + (y + dy + RING) % RING) * RING + (x + dx + RING) % RING) * 2 + core


def z_chip(shift):
    plane = 2 * RING * RING
    me = lax.axis_index("dp")
    place = (me // plane) * SHARED_KV_NUM + lax.axis_index("tensor") + shift
    place = (place + 2 * SHARED_KV_NUM) % (2 * SHARED_KV_NUM)
    return (place // SHARED_KV_NUM) * plane + me % plane, place % SHARED_KV_NUM


def greet():
    barrier = pltpu.get_barrier_semaphore()
    tensor = lax.axis_index("tensor")
    partners = [
        (neighbour_index(0, 0, 1), tensor),
        (neighbour_index(0, 0, -1), tensor),
        (neighbour_index(0, 1, 0), tensor),
        (neighbour_index(0, -1, 0), tensor),
        (neighbour_index(0, 0, 0, True), tensor),
        z_chip(Z_STEP),
        z_chip(-Z_STEP),
    ]
    for partner in partners:
        pl.semaphore_signal(
            barrier, inc=1, device_id=partner, device_id_type=pl.DeviceIdType.MESH
        )
    pl.semaphore_wait(barrier, len(partners))


def spread(source, slot, relay, send_sem, recv_sem, relay_sem, share, middle, after=None):
    me = lax.axis_index("dp")
    core = me % 2
    tensor = lax.axis_index("tensor")
    index = neighbour_index

    def along(half, dz, first, second):
        return index(dz, second, first) if half == 0 else index(dz, first, second)

    sibling = index(0, 0, 0, True)
    sent = []

    def push(src, dst, target, arrival):
        copy = pltpu.make_async_remote_copy(
            src_ref=src,
            dst_ref=dst,
            send_sem=send_sem.at[len(sent)],
            recv_sem=arrival,
            device_id=target,
            device_id_type=pl.DeviceIdType.MESH,
        )
        copy.start()
        sent.append(copy)

    def landed(there, arrival):
        pltpu.make_async_copy(there, there, arrival).wait()

    def forward(src, half, dz, first, second):
        origin = along(half, dz, first, second)

        def give(dfirst, dsecond):
            target = (along(half, 0, dfirst, dsecond), tensor)
            push(src, slot(origin, half), target, recv_sem.at[origin, half])

        if second == 0:
            if first == 0:
                give(1, 0)
                give(-1, 0)
            if first == -1 and dz == 0:
                give(1, 0)
            if first == 1 and dz == 1:
                give(-1, 0)
            give(0, 1)
            give(0, -1)
        upward = (abs(first) + dz) % 2 == 0
        if second == -1 and upward:
            give(0, 1)
        if second == 1 and not upward:
            give(0, -1)
        if share:
            push(src, slot(origin, half), (sibling, tensor), recv_sem.at[origin, half])

    offsets = [(f, s) for f in (0, -1, 1, 2) for s in (0, -1, 1, 2)]
    offsets.sort(key=lambda pair: abs(pair[0]) + abs(pair[1]))

    def receive(dz, hops):
        for first, second in offsets:
            if abs(first) + abs(second) == hops:
                for half in range(2):
                    origin = along(half, dz, first, second)
                    landed(slot(origin, half), recv_sem.at[origin, half])
                    forward(slot(origin, half), half, dz, first, second)

    def from_sibling(dz, lanes=(0, -1, 1, 2)):
        for first, second in offsets:
            for half in range(2):
                if (second if half == 0 else first) not in lanes:
                    continue
                origin = along(half, dz, first, second) + 1 - 2 * core
                landed(slot(origin, half), recv_sem.at[origin, half])

    for half in range(2):
        push(source(half), relay.at[half], z_chip(Z_STEP - 2 * Z_STEP * half), relay_sem.at[half])
    for half in range(2):
        forward(source(half), half, 0, 0, 0)
    receive(0, 1)
    for half in range(2):
        shift = Z_STEP - 2 * Z_STEP * half
        origin, _ = z_chip(-shift)
        landed(relay.at[half], relay_sem.at[half])
        push(relay.at[half], slot(origin, half), z_chip(shift), recv_sem.at[origin, half])
    for hops in range(2, 5):
        receive(0, hops)
    middle(from_sibling)
    for hops in range(5):
        receive(1, hops)
        if after is not None:
            after(hops, from_sibling)
    for copy in sent:
        copy.wait_send()


Z_STEP = 4
SENDS = 2 * (2 + 2 * (3 + 12))
SHARED_SENDS = SENDS + 2 * 2 * 16


def layer_kernel(
    normed_ref, block_ref, cos_ref, sin_ref, start_ref, kv_ref, mix_ref,
    weights, landing, both, landing_kv, tokens, mapped, made, parts,
    send_sem, recv_sem, relay_sem, send_kv, recv_kv, relay_kv, pair_send, pair_recv, local_sem,
):
    lines, width = block_ref.shape
    part = width // 2
    rows = kv_ref.shape[1]
    dim = PER_ATTN_DIM
    me = lax.axis_index("dp")
    core = me % 2
    heads = part // dim

    greet()

    def pair(src, dst, number):
        copy = pltpu.make_async_remote_copy(
            src_ref=src,
            dst_ref=dst,
            send_sem=pair_send.at[number],
            recv_sem=pair_recv.at[number],
            device_id=(neighbour_index(0, 0, 0, True), lax.axis_index("tensor")),
            device_id_type=pl.DeviceIdType.MESH,
        )
        copy.start()
        return copy

    def slot(origin, half):
        row = (origin // 2 * 2 + half) * lines
        return weights.at[pl.ds(pl.multiple_of(row, lines), lines), :]

    own = weights.at[pl.ds(pl.multiple_of(me * lines, lines), lines), :]
    block_swap = pair(
        block_ref.at[:, pl.ds(pl.multiple_of((1 - core) * part, part), part)], own, 0
    )
    keep = pltpu.make_async_copy(
        block_ref.at[:, pl.ds(pl.multiple_of(core * part, part), part)], own, local_sem.at[0]
    )
    keep.start()
    seat = tokens.at[pl.ds(pl.multiple_of(core * rows, rows), rows), :]
    token_swap = pair(normed_ref, seat, 1)
    keep_tokens = pltpu.make_async_copy(normed_ref, seat, local_sem.at[1])
    keep_tokens.start()
    keep.wait()
    block_swap.wait_recv()

    reach = normed_ref.shape[1] // 2
    plane = me // (2 * RING * RING)

    def product(which):
        place = pl.ds(pl.multiple_of(which * reach, reach), reach)
        return jnp.dot(
            tokens[:, place], weights[place, :], preferred_element_type=jnp.float32
        )

    def near(_):
        keep_tokens.wait()
        token_swap.wait_recv()
        mapped[...] = product(plane)

    spread(
        lambda half: slot(me, half),
        slot, landing, send_sem, recv_sem, relay_sem, False, near,
    )
    block_swap.wait_send()
    token_swap.wait_send()

    result = mapped[...] + product(1 - plane)
    for j in range(heads):
        vec = result[:, j * dim : (j + 1) * dim]
        spun = vec * cos_ref[...] + pltpu.roll(vec, dim // 2, 1) * sin_ref[...]
        if j == heads - 1:
            spun = jnp.where(core == 0, spun, vec)
        made[j] = spun.astype(jnp.bfloat16)
    theirs = pl.ds(pl.multiple_of((1 - core) * rows, rows), rows)
    ours = pl.ds(pl.multiple_of(core * rows, rows), rows)
    head_swap = pair(made.at[:, theirs, :], parts.at[pl.ds(core * heads, heads)], 2)
    for j in range(heads):
        parts[core * heads + j] = made[j, ours, :]
    head_swap.wait()

    def kv_slot(origin, half):
        return both.at[half, pl.ds(pl.multiple_of(origin * rows, rows), rows), :]

    mine = pl.ds(pl.multiple_of(me * rows, rows), rows)
    for half in range(2):
        kv_ref[half] = parts[QUARTET_SHARE + half]
        both[half, mine, :] = parts[QUARTET_SHARE + half]
    step = 512
    inv_root = 1.0 / math.sqrt(dim)
    total_rows = QUARTET_SHARE * rows
    q = parts[:QUARTET_SHARE].reshape(total_rows, dim)
    q_start = start_ref[...]
    q_index = me * rows + lax.broadcasted_iota(jnp.int32, (total_rows, 1), 0) % rows
    back = MAXLEN // rows
    low = (jnp.maximum(me - back, 0) * rows) // step
    high = ((me + 1) * rows + step - 1) // step

    def one_step(turn, state):
        top, total, accum = state
        begin = pl.multiple_of(turn * step, step)
        keys = both[0, pl.ds(begin, step), :]
        values = both[1, pl.ds(begin, step), :]
        key_index = begin + lax.broadcasted_iota(jnp.int32, (1, step), 1)
        allowed = (key_index <= q_index) & (key_index >= q_start)
        scores = (
            lax.dot_general(
                q, keys, (((1,), (1,)), ((), ())), preferred_element_type=jnp.float32
            )
            * inv_root
        )
        scores = jnp.where(allowed, scores, masked_score)
        new_top = jnp.maximum(top, jnp.max(scores, axis=1, keepdims=True))
        weight = jnp.exp(scores - new_top)
        fade = jnp.exp(top - new_top)
        total = total * fade + jnp.sum(weight, axis=1, keepdims=True)
        accum = accum * fade + jnp.dot(
            weight.astype(jnp.bfloat16), values, preferred_element_type=jnp.float32
        )
        return new_top, total, accum

    initial = (
        jnp.full((total_rows, 1), masked_score, jnp.float32),
        jnp.zeros((total_rows, 1), jnp.float32),
        jnp.zeros((total_rows, dim), jnp.float32),
    )
    state = [initial]

    def run(begin, end):
        count = jnp.maximum(end - begin, 0)
        state[0] = lax.fori_loop(
            0, count, lambda turn, held: one_step(end - 1 - turn, held), state[0]
        )

    half_steps = MAXLEN // step
    own_low = jnp.maximum(low, half_steps * plane)
    marks = [high] + [jnp.maximum(own_low, high - k) for k in (2, 3, 4, half_steps)]
    y = (me // (2 * RING)) % RING
    row_steps = half_steps // RING

    def far_row(dy):
        first_step = (y + dy + RING) % RING * row_steps
        run(jnp.maximum(first_step, low), jnp.minimum(first_step + row_steps, half_steps * plane))

    def near_keys(from_sibling):
        from_sibling(0)
        run(marks[1], marks[0])

    def far_keys(hops, from_sibling):
        if hops in (1, 2, 3):
            run(marks[hops + 1], marks[hops])
        if hops == 3:
            from_sibling(1, (0,))
            far_row(0)
        if hops == 4:
            from_sibling(1, (-1, 1))
            far_row(-1)
            far_row(1)
            from_sibling(1, (2,))
            far_row(2)

    spread(
        lambda half: parts.at[QUARTET_SHARE + half],
        kv_slot, landing_kv, send_kv, recv_kv, relay_kv, True, near_keys, far_keys,
    )
    top, total, accum = state[0]
    mix = (accum / total).astype(jnp.bfloat16)
    for j in range(QUARTET_SHARE):
        mix_ref[:, j * dim : (j + 1) * dim] = mix[j * rows : (j + 1) * rows]


def per_device(
    hidden, norm_gain, learner_probe_proj, learner_lookup_proj, learner_content_proj, lengths
):
    tok_rows = hidden.shape[0]
    learner_lines = learner_probe_proj.shape[0]
    group_width = (QUARTET_SHARE + 2) * PER_ATTN_DIM
    combined_slab = jnp.concatenate(
        [
            learner_probe_proj.reshape(learner_lines, SHARED_KV_NUM, QUARTET_SHARE * PER_ATTN_DIM),
            learner_lookup_proj.reshape(learner_lines, SHARED_KV_NUM, PER_ATTN_DIM),
            learner_content_proj.reshape(learner_lines, SHARED_KV_NUM, PER_ATTN_DIM),
        ],
        axis=2,
    )
    combined_slab = combined_slab.reshape(learner_lines, SHARED_KV_NUM * group_width).astype(
        jnp.bfloat16
    )
    serving_combined = lax.all_to_all(
        combined_slab, "tensor", split_axis=1, concat_axis=0, tiled=True
    )
    widened = hidden.astype(jnp.float32)
    scale = lax.rsqrt(jnp.mean(widened * widened, axis=1, keepdims=True) + norm_eps)
    normed = (widened * scale * norm_gain.astype(jnp.float32)[None, :]).astype(jnp.bfloat16)

    my_index = lax.axis_index("dp") * tok_rows + jnp.arange(tok_rows, dtype=jnp.int32)
    my_start = document_start(lengths, my_index)
    pair_index = (lax.axis_index("dp") // 2) * 2 * tok_rows + jnp.arange(
        2 * tok_rows, dtype=jnp.int32
    )
    pair_start = document_start(lengths, pair_index)
    half_dim = PER_ATTN_DIM // 2
    inverse = rope_theta ** (-2.0 * jnp.arange(half_dim, dtype=jnp.float32) / PER_ATTN_DIM)
    angles = (pair_index - pair_start).astype(jnp.float32)[:, None] * inverse[None, :]
    cosine = jnp.cos(angles)
    sine = jnp.sin(angles)
    cosine = jnp.concatenate([cosine, cosine], axis=1)
    sine = jnp.concatenate([-sine, sine], axis=1)

    rows = serving_combined.shape[0]
    devices = 4 * RING * RING
    part = group_width // 2
    starts = jnp.tile(my_start, QUARTET_SHARE)[:, None]
    vmem = pl.BlockSpec(memory_space=pltpu.VMEM)
    semaphores = []
    for sends in (SENDS, SHARED_SENDS):
        semaphores += [
            pltpu.SemaphoreType.DMA((sends,)),
            pltpu.SemaphoreType.DMA((devices, 2)),
            pltpu.SemaphoreType.DMA((2,)),
        ]
    semaphores += [
        pltpu.SemaphoreType.DMA((3,)),
        pltpu.SemaphoreType.DMA((3,)),
        pltpu.SemaphoreType.DMA((2,)),
    ]
    keys_values, attention_mix = pl.pallas_call(
        layer_kernel,
        out_shape=(
            jax.ShapeDtypeStruct((2, tok_rows, PER_ATTN_DIM), jnp.bfloat16),
            jax.ShapeDtypeStruct((tok_rows, QUARTET_SHARE * PER_ATTN_DIM), jnp.bfloat16),
        ),
        in_specs=[vmem] * 5,
        out_specs=(vmem, vmem),
        scratch_shapes=[
            pltpu.VMEM((rows * devices, part), jnp.bfloat16),
            pltpu.VMEM((2, rows, part), jnp.bfloat16),
            pltpu.VMEM((2, tok_rows * devices, PER_ATTN_DIM), jnp.bfloat16),
            pltpu.VMEM((2, tok_rows, PER_ATTN_DIM), jnp.bfloat16),
            pltpu.VMEM((2 * tok_rows, hidden.shape[1]), jnp.bfloat16),
            pltpu.VMEM((2 * tok_rows, part), jnp.float32),
            pltpu.VMEM((3, 2 * tok_rows, PER_ATTN_DIM), jnp.bfloat16),
            pltpu.VMEM((6, tok_rows, PER_ATTN_DIM), jnp.bfloat16),
        ]
        + semaphores,
        compiler_params=pltpu.CompilerParams(
            collective_id=0, has_side_effects=True, vmem_limit_bytes=48 * 2**20
        ),
        name="layer",
    )(normed, serving_combined, cosine, sine, starts)
    return (serving_combined, keys_values[0], keys_values[1], attention_mix)


def solution(mesh):
    in_specs = (
        P("dp", None),
        P(),
        P(("dp", "tensor"), None),
        P(("dp", "tensor"), None),
        P(("dp", "tensor"), None),
        P(),
    )
    out_specs = (P("dp", "tensor"), P("dp", "tensor"), P("dp", "tensor"), P("dp", "tensor"))
    return jax.shard_map(
        per_device, mesh=mesh, in_specs=in_specs, out_specs=out_specs, check_vma=False
    )
```
